256 devices in a mesh: tp: 16 (over x, z_lo), hb: 16 (over y, z_hi, core).
Axes of the slice: x: 4, y: 4, z: 8 (z_hi: 2, z_lo: 4; z = z_hi * 4 + z_lo), core: 2. Of those that a mesh axis runs over, the one named last changes fastest.
Arguments:
- normed: bfloat16 [2048, 16384], P('hb', 'tp'), may hold values from -6 to 6
- hidden: bfloat16 [2048, 26624], P('hb', 'tp'), may hold values from -6 to 6
Outputs:
- h_in: float32 [16384, 16384], P('tp', 'hb')
- h_down: float32 [26624, 1664], P(('tp', 'hb'))
The draws below stay inside these ranges and needn't reach their ends.
All inputs are finite; a program needn't handle non-finite values.
Results may differ from the reference program's by a relative error of at most 0.0003.
Values may be sent and summed in bfloat16 or wider, within the bound.
No kernel may reach another device: no remote copies, remote signals or barrier semaphores. Data moves between devices by JAX's collectives and lax.ppermute only.
A program may use at most 128 MiB of HBM per device.

```python
import jax
import jax.numpy as jnp
from jax import lax

D = 16384
FFW = 26624
TOKENS = 2048
N_TP = 16


def level_of(stream_key, shape, shards, least, high):
    factor_of = 1.0
    for position, shards_of in shards:
        heights = jax.random.uniform(jax.random.fold_in(jax.random.fold_in(stream_key, 6), position), (shards_of,), jnp.float32, least / len(shards), high / len(shards))
        factor_of = factor_of * jnp.repeat(jnp.exp(heights), shape[position] // shards_of).reshape((-1,) + (1,) * (len(shape) - 1 - position))
    return factor_of


def bell_draw(key, extent, spread, bound, cuts=(), kind=jnp.bfloat16):
    drawn = jax.random.normal(key, extent, jnp.float32) * spread
    if len(cuts) > 0:
        drawn = level_of(key, extent, cuts, -0.22, 0.18) * drawn
    return jnp.clip(drawn, min=-bound, max=bound).astype(kind)


def setup_inputs(seed: int = 0) -> dict:
    streams_of = jax.random.split(jax.random.key(seed), 3)
    normed = bell_draw(streams_of[0], (TOKENS, D), 1.0, 6.0, ((0, 16), (1, 16)))
    hidden = bell_draw(streams_of[1], (TOKENS, FFW), 1.0, 6.0, ((0, 16), (1, 16)))
    return {"normed": normed, "hidden": hidden}


def reference(normed, hidden):
    scale = 2.0 / TOKENS
    rows_in = normed.astype(jnp.float32)
    h_in = jnp.dot(rows_in.T, rows_in, precision=lax.Precision.HIGHEST) * scale
    units = hidden.astype(jnp.float32).reshape(TOKENS, N_TP, FFW // N_TP)
    blocks = jnp.einsum("tbi,tbj->bij", units, units, precision=lax.Precision.HIGHEST)
    h_down = blocks.reshape(FFW, FFW // N_TP) * scale
    return h_in, h_down
```

```python
import jax
import jax.numpy as jnp
from jax import lax
from jax.sharding import PartitionSpec as P


def gram_product(left, right):
    return lax.dot_general(
        left, right, (((0,), (0,)), ((), ())), preferred_element_type=jnp.float32
    )


def per_device(normed, hidden):
    groups = lax.axis_size("hb")
    scale = 2.0 / (normed.shape[0] * groups)
    swap = [(t * groups + h, h * groups + t) for t in range(groups) for h in range(groups)]
    moved = lax.ppermute(normed, ("tp", "hb"), swap)
    columns = lax.all_gather(moved, "tp", axis=0, tiled=True)
    rows = lax.all_gather(normed, "hb", axis=0, tiled=True)
    units = lax.all_gather(hidden, "hb", axis=0, tiled=True)
    h_in = gram_product(rows, columns) * scale
    width = hidden.shape[1] // groups
    mine = lax.dynamic_slice_in_dim(units, lax.axis_index("hb") * width, width, axis=1)
    h_down = gram_product(mine, units) * scale
    return (h_in, h_down)


def solution(mesh):
    return jax.shard_map(
        per_device,
        mesh=mesh,
        in_specs=(P("hb", "tp"), P("hb", "tp")),
        out_specs=(P("tp", "hb"), P(("tp", "hb"), None)),
        check_vma=False,
    )
```

```python
import functools
import itertools

import jax
import jax.numpy as jnp
from jax import lax
from jax.experimental import pallas as pl
from jax.experimental.pallas import tpu as pltpu
from jax.sharding import PartitionSpec as P

SIZES = (4, 4, 4, 2, 2)
LOOP = (1, 3, 0, 2)
BACK = (2, 0, 3, 1)
DOT = (((0,), (0,)), ((), ()))


def linear(place):
    index = 0
    for part, size in zip(place, SIZES):
        index = index * size + part % size
    return index


def send(value, target):
    pairs = [
        (linear(place), linear(target(*place)))
        for place in itertools.product(*map(range, SIZES))
    ]
    return lax.ppermute(value, ("tp", "hb"), pairs)


def send_y(value, step):
    return send(value, lambda x, zl, y, zh, c: (x, zl, y + step, zh, c))


def send_x(value, step):
    return send(value, lambda x, zl, y, zh, c: (x + step, zl, y, zh, c))


def other_zh(value):
    return send(value, lambda x, zl, y, zh, c: (x, zl, y, 1 - zh, c))


def other_core(value):
    return send(value, lambda x, zl, y, zh, c: (x, zl, y, zh, 1 - c))


def transpose(value):
    return send(
        value,
        lambda x, zl, y, zh, c: (x + y, zh * 2 + (c ^ (zl & 1)), x, zl >> 1, zl & 1),
    )


def along(value, send_axis, way):
    below, above = send_axis(value, 1), send_axis(value, -1)
    far = send_axis(below, 1) if way > 0 else send_axis(above, -1)
    return [(0, value), (-1, below), (1, above), (2, far)]


def place_of():
    tp, hb = lax.axis_index("tp"), lax.axis_index("hb")
    return tp // 4, tp % 4, hb // 4, hb // 2 % 2, hb % 2


def row_blocks(value):
    found = []
    _, _, y, zh, c = place_of()
    for flip, block in enumerate((value, other_zh(value))):
        for offset, part in along(block, send_y, 1 - 2 * flip):
            for swap, piece in enumerate((part, other_core(part))):
                token = (y + offset) % 4 * 4 + (zh ^ flip) * 2 + (c ^ swap)
                found.append((token, piece))
    return found


def column_blocks(value):
    found = []
    x, zl, y, _, c = place_of()
    block = transpose(value)
    for step in range(4):
        for offset, part in along(block, send_x, 1 - 2 * (step % 2)):
            token = (x + offset - y) % 4 * 4 + (zl >> 1) * 2 + ((zl & 1) ^ c)
            found.append((token, part))
        if step < 3:
            block = send(block, lambda x, zl, y, zh, c: (x, LOOP[zl], y, zh, c))
            zl = jnp.array(BACK, jnp.int32)[zl]
    return found


def rows_kernel(count, scale, slots, *refs):
    blocks, out = refs[: 2 * count], refs[2 * count]
    left, right, sems = refs[2 * count + 1 :]
    tokens = blocks[0].shape[0]
    copies = []
    for k, block in enumerate(blocks):
        panel = left if k < count else right
        start = pl.multiple_of(slots[k] * tokens, tokens)
        copies.append(
            pltpu.make_async_copy(block, panel.at[pl.ds(start, tokens), :], sems.at[k])
        )
        copies[-1].start()
    for copy in copies:
        copy.wait()
    tile = 256
    for m in range(out.shape[0] // tile):
        at = slice(m * tile, (m + 1) * tile)
        out[at, :] = scale * lax.dot_general(
            left[:, at], right[...], DOT, preferred_element_type=jnp.float32
        )


def in_product(rows, columns, scale):
    count = len(rows)
    tokens, width = rows[0][1].shape
    blocks = [block for _, block in rows + columns]
    slots = jnp.stack([token for token, _ in rows + columns]).astype(jnp.int32)
    return pl.pallas_call(
        functools.partial(rows_kernel, count, scale),
        out_shape=jax.ShapeDtypeStruct((width, width), jnp.float32),
        in_specs=[pl.BlockSpec(memory_space=pltpu.SMEM)]
        + [pl.BlockSpec(memory_space=pl.ANY)] * (2 * count),
        out_specs=pl.BlockSpec(memory_space=pltpu.VMEM),
        scratch_shapes=[
            pltpu.VMEM((count * tokens, width), jnp.bfloat16),
            pltpu.VMEM((count * tokens, width), jnp.bfloat16),
            pltpu.SemaphoreType.DMA((2 * count,)),
        ],
        compiler_params=pltpu.CompilerParams(vmem_limit_bytes=32 << 20),
        cost_estimate=pl.CostEstimate(
            flops=2 * count * tokens * width * width,
            bytes_accessed=12 << 20,
            transcendentals=0,
        ),
    )(slots, *blocks)


def down_kernel(count, scale, own, *refs):
    blocks, out = refs[:count], refs[count]
    panel, sems = refs[count + 1 :]
    tokens = blocks[0].shape[0]
    copies = []
    for k, block in enumerate(blocks):
        at = pl.ds(k * tokens, tokens)
        copies.append(pltpu.make_async_copy(block, panel.at[at, :], sems.at[k]))
        copies[-1].start()
    rows, width = out.shape
    start = own[0] * rows
    base = jnp.minimum(start // 128 * 128, width - 256)
    base = pl.multiple_of(base, 128)
    pick = lax.broadcasted_iota(jnp.int32, (256, rows), 0) == (
        start - base + lax.broadcasted_iota(jnp.int32, (256, rows), 1)
    )
    for copy in copies:
        copy.wait()
    mine = jnp.dot(
        panel[:, pl.ds(base, 256)],
        pick.astype(jnp.float32).astype(jnp.bfloat16),
        preferred_element_type=jnp.float32,
    ).astype(jnp.bfloat16)
    out[...] = scale * lax.dot_general(
        mine, panel[...], DOT, preferred_element_type=jnp.float32
    )


def down_product(units, scale):
    count = len(units)
    tokens, width = units[0].shape
    rows = width // count
    return pl.pallas_call(
        functools.partial(down_kernel, count, scale),
        out_shape=jax.ShapeDtypeStruct((rows, width), jnp.float32),
        in_specs=[pl.BlockSpec(memory_space=pltpu.SMEM)]
        + [pl.BlockSpec(memory_space=pl.ANY)] * count,
        out_specs=pl.BlockSpec(memory_space=pltpu.VMEM),
        scratch_shapes=[
            pltpu.VMEM((count * tokens, width), jnp.bfloat16),
            pltpu.SemaphoreType.DMA((count,)),
        ],
        compiler_params=pltpu.CompilerParams(vmem_limit_bytes=24 << 20),
        cost_estimate=pl.CostEstimate(
            flops=2 * count * tokens * rows * width,
            bytes_accessed=8 << 20,
            transcendentals=0,
        ),
    )(lax.axis_index("hb").astype(jnp.int32)[None], *units)


def per_device(normed, hidden):
    groups = lax.axis_size("hb")
    scale = 2.0 / (normed.shape[0] * groups)
    columns = column_blocks(normed)
    rows = row_blocks(normed)
    units = [block for _, block in row_blocks(hidden)]
    h_in = in_product(rows, columns, scale)
    h_down = down_product(units, scale)
    return (h_in, h_down)


def solution(mesh):
    return jax.shard_map(
        per_device,
        mesh=mesh,
        in_specs=(P("hb", "tp"), P("hb", "tp")),
        out_specs=(P("tp", "hb"), P(("tp", "hb"), None)),
        check_vma=False,
    )
```

```python
import functools
import itertools

import jax
import jax.numpy as jnp
from jax import lax
from jax.experimental import pallas as pl
from jax.experimental.pallas import tpu as pltpu
from jax.sharding import PartitionSpec as P

SIZES = (4, 4, 4, 2, 2)
LOOP = (1, 3, 0, 2)
DOT = (((0,), (0,)), ((), ()))
VMEM = pl.BlockSpec(memory_space=pltpu.VMEM)


def linear(place):
    index = 0
    for part, size in zip(place, SIZES):
        index = index * size + part % size
    return index


def send(value, target):
    pairs = [
        (linear(place), linear(target(*place)))
        for place in itertools.product(*map(range, SIZES))
    ]
    return lax.ppermute(value, ("tp", "hb"), pairs)


def up_y(x, zl, y, zh, c):
    return x, zl, y + 1, zh, c


def down_y(x, zl, y, zh, c):
    return x, zl, y - 1, zh, c


def up_x(x, zl, y, zh, c):
    return x + 1, zl, y, zh, c


def down_x(x, zl, y, zh, c):
    return x - 1, zl, y, zh, c


def other_zh(x, zl, y, zh, c):
    return x, zl, y, 1 - zh, c


def other_core(x, zl, y, zh, c):
    return x, zl, y, zh, 1 - c


def next_zl(x, zl, y, zh, c):
    return x, LOOP[zl], y, zh, c


def last_zl(x, zl, y, zh, c):
    return x, LOOP.index(zl), y, zh, c


SPREAD = ((0, 1, 3, 2), (1, 2, 0, 3), (3, 0, 2, 1), (0, 1, 3, 2))
ORIGIN = [0, 0]
for _old, _row in enumerate(SPREAD):
    for _token, _new in enumerate(_row):
        ORIGIN[_old // 2] |= _token << 2 * (_old % 2 * 4 + _new)


def transpose(x, zl, y, zh, c):
    return x + y, SPREAD[zl][zh * 2 + c], x, zl >> 1, zl & 1


class Steps:
    def __init__(self):
        self.last = ()

    def hold(self, *values):
        if self.last:
            values = lax.optimization_barrier((*values, *self.last))[: len(values)]
        return values

    def __call__(self, *moves, slow=0):
        values = self.hold(*(value for value, _ in moves))
        results = [send(value, target) for value, (_, target) in zip(values, moves)]
        self.last = results[slow:]
        return results


def place_of():
    tp, hb = lax.axis_index("tp"), lax.axis_index("hb")
    return tp // 4, tp % 4, hb // 4, hb // 2 % 2, hb % 2


OFFSETS = (0, -1, 1, 2)


def copy_all(pairs, sems):
    copies = [
        pltpu.make_async_copy(source, target, sems.at[k])
        for k, (source, target) in enumerate(pairs)
    ]
    for copy in copies:
        copy.start()
    return copies


def rows_kernel(*refs):
    blocks, panel, sems = refs[:8], refs[8], refs[9]
    _, _, y, zh, _ = place_of()
    pairs = []
    for flip in range(2):
        for offset, block in zip(OFFSETS, blocks[4 * flip : 4 * flip + 4]):
            slot = (y + offset + 4) % 4 * 2 + (zh ^ flip)
            pairs.append((block, panel.at[slot]))
    for copy in copy_all(pairs, sems):
        copy.wait()


def rows_panel(blocks):
    return pl.pallas_call(
        rows_kernel,
        out_shape=jax.ShapeDtypeStruct((8, *blocks[0].shape), blocks[0].dtype),
        in_specs=[VMEM] * 8,
        out_specs=VMEM,
        scratch_shapes=[pltpu.SemaphoreType.DMA((8,))],
        compiler_params=pltpu.CompilerParams(vmem_limit_bytes=4 << 20),
        cost_estimate=pl.CostEstimate(
            flops=0, bytes_accessed=1 << 20, transcendentals=0
        ),
    )(*blocks)


def in_kernel(scale, *refs):
    own, other = refs[:2]
    blocks, out, panel, tiles, sems, out_sems = refs[2:18], *refs[18:]
    x, zl, y, zh, c = place_of()
    codes = jnp.where(zh == 0, ORIGIN[0], ORIGIN[1]) >> 8 * c
    tokens = own.shape[1]
    pairs = []
    for step in range(4):
        for offset, block in zip(OFFSETS, blocks[4 * step : 4 * step + 4]):
            group = codes >> 2 * zl & 3
            slot = (x + offset - y + 8) % 4 * 2 + (group >> 1) + 8 * (group & 1 ^ c)
            at = pl.ds(pl.multiple_of(slot * tokens, tokens), tokens)
            pairs.append((block, panel.at[at, :]))
        zl = jnp.where(zl == 0, 2, jnp.where(zl == 1, 0, jnp.where(zl == 2, 3, 1)))
    for copy in copy_all(pairs, sems):
        copy.wait()
    half, width = 8 * tokens, out.shape[1]
    tile = tiles.shape[1]
    writes = []
    for m in range(out.shape[0] // tile):
        at = slice(m * tile, (m + 1) * tile)
        if m > 1:
            writes[m - 2].wait()
        left = jnp.concatenate(
            [part[:, :, at].reshape(half, tile) for part in (own, other)], axis=0
        )
        tiles[m % 2] = scale * lax.dot_general(
            left, panel[...], DOT, preferred_element_type=jnp.float32
        )
        writes.append(
            pltpu.make_async_copy(tiles.at[m % 2], out.at[at, :], out_sems.at[m % 2])
        )
        writes[-1].start()
    for write in writes[-2:]:
        write.wait()


def in_product(own, other, blocks, scale):
    tokens, width = blocks[0].shape
    count = len(blocks)
    return pl.pallas_call(
        functools.partial(in_kernel, scale),
        out_shape=jax.ShapeDtypeStruct((width, width), jnp.float32),
        in_specs=[VMEM] * (2 + count),
        out_specs=pl.BlockSpec(memory_space=pl.ANY),
        scratch_shapes=[
            pltpu.VMEM((count * tokens, width), jnp.bfloat16),
            pltpu.VMEM((2, width // 4, width), jnp.float32),
            pltpu.SemaphoreType.DMA((count,)),
            pltpu.SemaphoreType.DMA((2,)),
        ],
        compiler_params=pltpu.CompilerParams(vmem_limit_bytes=24 << 20),
        cost_estimate=pl.CostEstimate(
            flops=2 * count * tokens * width * width,
            bytes_accessed=12 << 20,
            transcendentals=0,
        ),
    )(own, other, *blocks)


def down_kernel(scale, *refs):
    blocks, mine, theirs, panel, sems = refs[:8], *refs[8:]
    tokens = blocks[0].shape[0]
    copies = copy_all(
        [(block, panel.at[pl.ds(k * tokens, tokens), :]) for k, block in enumerate(blocks)],
        sems,
    )
    rows, width = mine.shape
    group = lax.axis_index("hb")
    span = 384
    base = jnp.minimum(group // 2 * 2 * rows // 128 * 128, width - span)
    base = pl.multiple_of(base, 128)
    lane = lax.broadcasted_iota(jnp.int32, (span, 256), 1)
    owner = jnp.where(lane < 128, group, group ^ 1)
    wanted = owner * rows - base + (lane & 127)
    pick = lax.broadcasted_iota(jnp.int32, (span, 256), 0) == wanted
    for copy in copies:
        copy.wait()
    left = jnp.dot(
        panel[:, pl.ds(base, span)],
        jnp.where(pick, 1.0, 0.0).astype(jnp.bfloat16),
        preferred_element_type=jnp.float32,
    ).astype(jnp.bfloat16)
    both = scale * lax.dot_general(
        left, panel[...], DOT, preferred_element_type=jnp.float32
    )
    mine[...] = both[:rows]
    theirs[...] = both[128 : 128 + rows]


def down_terms(blocks, scale):
    tokens, width = blocks[0].shape
    rows = width // lax.axis_size("hb")
    term = jax.ShapeDtypeStruct((rows, width), jnp.float32)
    return pl.pallas_call(
        functools.partial(down_kernel, scale),
        out_shape=(term, term),
        in_specs=[VMEM] * 8,
        out_specs=(VMEM, VMEM),
        scratch_shapes=[
            pltpu.VMEM((8 * tokens, width), jnp.bfloat16),
            pltpu.SemaphoreType.DMA((8,)),
        ],
        compiler_params=pltpu.CompilerParams(vmem_limit_bytes=16 << 20),
        cost_estimate=pl.CostEstimate(
            flops=2 * 8 * tokens * 256 * width,
            bytes_accessed=6 << 20,
            transcendentals=0,
        ),
    )(*blocks)


def per_device(normed, hidden):
    scale = 2.0 / (normed.shape[0] * lax.axis_size("hb"))
    step = Steps()
    first, normed_1, n_below, n_above, h_below = step(
        (normed, transpose), (normed, other_zh), (normed, up_y), (normed, down_y), (hidden, up_y)
    )
    second, fourth, x_below_0, x_above_0, h_above = step(
        (first, next_zl), (first, last_zl), (first, up_x), (first, down_x), (hidden, down_y)
    )
    hidden_1, third, x_below_1, x_above_1, n_below_1, n_above_1 = step(
        (hidden, other_zh), (second, next_zl), (second, up_x), (second, down_x),
        (normed_1, up_y), (normed_1, down_y), slow=1,
    )
    x_below_3, x_above_3, x_below_2, x_above_2, n_far, n_far_1 = step(
        (fourth, up_x), (fourth, down_x), (third, up_x), (third, down_x),
        (n_below, up_y), (n_above_1, down_y)
    )
    own = rows_panel(
        [normed, n_below, n_above, n_far, normed_1, n_below_1, n_above_1, n_far_1]
    )
    h_below_1, h_above_1, x_far_0, x_far_1, other = step(
        (hidden_1, up_y), (hidden_1, down_y), (x_below_0, up_x), (x_above_1, down_x),
        (own, other_core)
    )
    h_far_1, h_far, x_far_2, x_far_3 = step(
        (h_above_1, down_y), (h_below, up_y), (x_below_2, up_x), (x_above_3, down_x)
    )
    mine, theirs = down_terms(
        step.hold(hidden, h_below, h_above, h_far, hidden_1, h_below_1, h_above_1, h_far_1),
        scale,
    )
    columns = [
        first, x_below_0, x_above_0, x_far_0,
        second, x_below_1, x_above_1, x_far_1,
        third, x_below_2, x_above_2, x_far_2,
        fourth, x_below_3, x_above_3, x_far_3,
    ]
    h_down = mine + send(theirs, other_core)
    h_in = in_product(own, other, columns, scale)
    return (h_in, h_down)


def solution(mesh):
    return jax.shard_map(
        per_device,
        mesh=mesh,
        in_specs=(P("hb", "tp"), P("hb", "tp")),
        out_specs=(P("tp", "hb"), P(("tp", "hb"), None)),
        check_vma=False,
    )
```

```python
import functools
import itertools

import jax
import jax.numpy as jnp
from jax import lax
from jax.experimental import pallas as pl
from jax.experimental.pallas import tpu as pltpu
from jax.sharding import PartitionSpec as P

SIZES = (4, 4, 4, 2, 2)
LOOP = (1, 3, 0, 2)
DOT = (((0,), (0,)), ((), ()))
VMEM = pl.BlockSpec(memory_space=pltpu.VMEM)


def linear(place):
    index = 0
    for part, size in zip(place, SIZES):
        index = index * size + part % size
    return index


def send(value, target):
    pairs = [
        (linear(place), linear(target(*place)))
        for place in itertools.product(*map(range, SIZES))
    ]
    return lax.ppermute(value, ("tp", "hb"), pairs)


def up_y(x, zl, y, zh, c):
    return x, zl, y + 1, zh, c


def down_y(x, zl, y, zh, c):
    return x, zl, y - 1, zh, c


def up_x(x, zl, y, zh, c):
    return x + 1, zl, y, zh, c


def down_x(x, zl, y, zh, c):
    return x - 1, zl, y, zh, c


def other_zh(x, zl, y, zh, c):
    return x, zl, y, 1 - zh, c


def other_core(x, zl, y, zh, c):
    return x, zl, y, zh, 1 - c


def next_zl(x, zl, y, zh, c):
    return x, LOOP[zl], y, zh, c


def last_zl(x, zl, y, zh, c):
    return x, LOOP.index(zl), y, zh, c


SPREAD = ((0, 1, 3, 2), (1, 2, 0, 3), (3, 0, 2, 1), (0, 1, 3, 2))
ORIGIN = [0, 0]
for _old, _row in enumerate(SPREAD):
    for _token, _new in enumerate(_row):
        ORIGIN[_old // 2] |= _token << 2 * (_old % 2 * 4 + _new)


def transpose(x, zl, y, zh, c):
    return x + y, SPREAD[zl][zh * 2 + c], x, zl >> 1, zl & 1


class Steps:
    def __init__(self):
        self.last = ()

    def hold(self, *values):
        if self.last:
            values = lax.optimization_barrier((*values, *self.last))[: len(values)]
        return values

    def __call__(self, *moves, slow=0):
        values = self.hold(*(value for value, _ in moves))
        results = [send(value, target) for value, (_, target) in zip(values, moves)]
        self.last = results[slow:]
        return results


def place_of():
    tp, hb = lax.axis_index("tp"), lax.axis_index("hb")
    return tp // 4, tp % 4, hb // 4, hb // 2 % 2, hb % 2


OFFSETS = (0, -1, 1, 2)


def copy_all(pairs, sems):
    copies = [
        pltpu.make_async_copy(source, target, sems.at[k])
        for k, (source, target) in enumerate(pairs)
    ]
    for copy in copies:
        copy.start()
    return copies


def rows_kernel(*refs):
    blocks, panel, sems = refs[:8], refs[8], refs[9]
    _, _, y, zh, _ = place_of()
    pairs = []
    for flip in range(2):
        for offset, block in zip(OFFSETS, blocks[4 * flip : 4 * flip + 4]):
            slot = (y + offset + 4) % 4 * 2 + (zh ^ flip)
            pairs.append((block, panel.at[slot]))
    for copy in copy_all(pairs, sems):
        copy.wait()


def rows_panel(blocks):
    return pl.pallas_call(
        rows_kernel,
        out_shape=jax.ShapeDtypeStruct((8, *blocks[0].shape), blocks[0].dtype),
        in_specs=[pl.BlockSpec(memory_space=pl.ANY)] + [VMEM] * 7,
        out_specs=VMEM,
        scratch_shapes=[pltpu.SemaphoreType.DMA((8,))],
        compiler_params=pltpu.CompilerParams(vmem_limit_bytes=4 << 20),
        cost_estimate=pl.CostEstimate(
            flops=0, bytes_accessed=1 << 20, transcendentals=0
        ),
    )(*blocks)


def in_kernel(steps, scale, *refs):
    own, other = refs[:2]
    blocks = refs[2 : 2 + 4 * len(steps)]
    left, right, tiles, sems, out_sems = refs[-5:]
    out, before = refs[-6], refs[2 + 4 * len(steps) : -6]
    x, zl, y, zh, c = place_of()
    codes = jnp.where(zh == 0, ORIGIN[0], ORIGIN[1]) >> 8 * c
    tokens = own.shape[1]
    copies = []
    for step in range(4):
        group = codes >> 2 * zl & 3
        swap = group & 1 ^ c
        for k, offset in enumerate(OFFSETS if step in steps else ()):
            at = 4 * steps.index(step) + k
            rows = pl.ds(at * tokens, tokens)
            slot = (x + offset - y + 8) % 4 * 2 + (group >> 1)
            copies.append(
                pltpu.make_async_copy(blocks[at], right.at[rows, :], sems.at[0, at])
            )
            copies[-1].start()
            near = pltpu.make_async_copy(own.at[slot], left.at[rows, :], sems.at[1, at])
            far = pltpu.make_async_copy(other.at[slot], left.at[rows, :], sems.at[1, at])
            pl.when(swap == 0)(near.start)
            pl.when(swap == 1)(far.start)
            copies.append(near)
        zl = jnp.where(zl == 0, 2, jnp.where(zl == 1, 0, jnp.where(zl == 2, 3, 1)))
    for copy in copies:
        copy.wait()
    tile = tiles.shape[1]
    writes = []
    for m in range(out.shape[0] // tile):
        at = slice(m * tile, (m + 1) * tile)
        part = scale * lax.dot_general(
            left[:, at], right[...], DOT, preferred_element_type=jnp.float32
        )
        if not before:
            out[at, :] = part
            continue
        if m > 1:
            writes[m - 2].wait()
        tiles[m % 2] = before[0][at, :] + part
        writes.append(
            pltpu.make_async_copy(tiles.at[m % 2], out.at[at, :], out_sems.at[m % 2])
        )
        writes[-1].start()
    for write in writes[-2:]:
        write.wait()


def in_product(own, other, blocks, steps, scale, before=()):
    tokens, width = blocks[0].shape
    count = len(blocks)
    return pl.pallas_call(
        functools.partial(in_kernel, steps, scale),
        out_shape=jax.ShapeDtypeStruct((width, width), jnp.float32),
        in_specs=[VMEM] * (2 + count + len(before)),
        out_specs=pl.BlockSpec(memory_space=pl.ANY) if before else VMEM,
        scratch_shapes=[
            pltpu.VMEM((count * tokens, width), jnp.bfloat16),
            pltpu.VMEM((count * tokens, width), jnp.bfloat16),
            pltpu.VMEM((2, width // 4, width), jnp.float32),
            pltpu.SemaphoreType.DMA((2, count)),
            pltpu.SemaphoreType.DMA((2,)),
        ],
        compiler_params=pltpu.CompilerParams(vmem_limit_bytes=20 << 20),
        cost_estimate=pl.CostEstimate(
            flops=2 * count * tokens * width * width,
            bytes_accessed=8 << 20,
            transcendentals=0,
        ),
    )(own, other, *blocks, *before)


def down_kernel(count, scale, *refs):
    blocks, before = refs[:count], refs[count:-4]
    mine, theirs, panel, sems = refs[-4:]
    pairs, start = [], 0
    for block in blocks:
        stop = start + block.shape[0]
        pairs.append((block, panel.at[start:stop, :]))
        start = stop
    copies = copy_all(pairs, sems)
    rows, width = mine.shape
    group = lax.axis_index("hb")
    span = 384
    base = jnp.minimum(group // 2 * 2 * rows // 128 * 128, width - span)
    base = pl.multiple_of(base, 128)
    lane = lax.broadcasted_iota(jnp.int32, (span, 256), 1)
    owner = jnp.where(lane < 128, group, group ^ 1)
    wanted = owner * rows - base + (lane & 127)
    pick = lax.broadcasted_iota(jnp.int32, (span, 256), 0) == wanted
    for copy in copies:
        copy.wait()
    left = jnp.dot(
        panel[:, pl.ds(base, span)],
        jnp.where(pick, 1.0, 0.0).astype(jnp.bfloat16),
        preferred_element_type=jnp.float32,
    ).astype(jnp.bfloat16)
    both = scale * lax.dot_general(
        left, panel[...], DOT, preferred_element_type=jnp.float32
    )
    for term, at in ((mine, 0), (theirs, 128)):
        part = both[at : at + rows]
        term[...] = part if not before else before[at // 128][...] + part


def down_terms(blocks, scale, before=()):
    width = blocks[0].shape[1]
    tokens = sum(block.shape[0] for block in blocks)
    rows = width // lax.axis_size("hb")
    term = jax.ShapeDtypeStruct((rows, width), jnp.float32)
    first = VMEM if before else pl.BlockSpec(memory_space=pl.ANY)
    return pl.pallas_call(
        functools.partial(down_kernel, len(blocks), scale),
        out_shape=(term, term),
        in_specs=[first] + [VMEM] * (len(blocks) - 1 + len(before)),
        out_specs=(VMEM, VMEM),
        scratch_shapes=[
            pltpu.VMEM((tokens, width), jnp.bfloat16),
            pltpu.SemaphoreType.DMA((len(blocks),)),
        ],
        compiler_params=pltpu.CompilerParams(vmem_limit_bytes=16 << 20),
        cost_estimate=pl.CostEstimate(
            flops=2 * tokens * 256 * width,
            bytes_accessed=6 << 20,
            transcendentals=0,
        ),
    )(*blocks, *before)


def per_device(normed, hidden):
    scale = 2.0 / (normed.shape[0] * lax.axis_size("hb"))
    step = Steps()
    first, normed_1, h_below, h_above = step(
        (normed, transpose), (normed, other_zh), (hidden, up_y), (hidden, down_y)
    )
    second, fourth, x_below_0, x_above_0, n_below, n_above = step(
        (first, next_zl), (first, last_zl), (first, up_x), (first, down_x),
        (normed, up_y), (normed, down_y)
    )
    hidden_1, third, x_below_1, x_above_1, n_below_1, n_above_1 = step(
        (hidden, other_zh), (second, next_zl), (second, up_x), (second, down_x),
        (normed_1, up_y), (normed_1, down_y), slow=1,
    )
    x_below_3, x_above_3, x_below_2, x_above_2, n_far, n_far_1 = step(
        (fourth, up_x), (fourth, down_x), (third, up_x), (third, down_x),
        (n_below, up_y), (n_above_1, down_y)
    )
    own = rows_panel(
        [normed, n_below, n_above, n_far, normed_1, n_below_1, n_above_1, n_far_1]
    )
    h_below_1, h_above_1, x_far_0, x_far_1, other = step(
        (hidden_1, up_y), (hidden_1, down_y), (x_below_0, up_x), (x_above_1, down_x),
        (own, other_core)
    )
    early = [first, x_below_0, x_above_0, x_far_0, second, x_below_1, x_above_1, x_far_1]
    partial = in_product(own, other, early, (0, 1), scale)
    terms = down_terms(
        [hidden, h_below, h_above, hidden_1, h_below_1, h_above_1], scale
    )
    h_far_1, h_far, x_far_2, x_far_3 = step(
        (h_above_1, down_y), (h_below, up_y), (x_below_2, up_x), (x_above_3, down_x)
    )
    *held, partial = step.hold(h_far, h_far_1, partial)
    mine, theirs = down_terms(held, scale, terms)
    h_down = mine + send(theirs, other_core)
    late = [third, x_below_2, x_above_2, x_far_2, fourth, x_below_3, x_above_3, x_far_3]
    h_in = in_product(own, other, late, (2, 3), scale, (partial,))
    return (h_in, h_down)


def solution(mesh):
    return jax.shard_map(
        per_device,
        mesh=mesh,
        in_specs=(P("hb", "tp"), P("hb", "tp")),
        out_specs=(P("tp", "hb"), P(("tp", "hb"), None)),
        check_vma=False,
    )
```

```python
import functools
import itertools

import jax
import jax.numpy as jnp
from jax import lax
from jax.experimental import pallas as pl
from jax.experimental.pallas import tpu as pltpu
from jax.sharding import PartitionSpec as P

SIZES = (4, 4, 4, 2, 2)
LOOP = (1, 3, 0, 2)
DOT = (((0,), (0,)), ((), ()))
VMEM = pl.BlockSpec(memory_space=pltpu.VMEM)


def linear(place):
    index = 0
    for part, size in zip(place, SIZES):
        index = index * size + part % size
    return index


def send(value, target):
    pairs = [
        (linear(place), linear(target(*place)))
        for place in itertools.product(*map(range, SIZES))
    ]
    return lax.ppermute(value, ("tp", "hb"), pairs)


def up_y(x, zl, y, zh, c):
    return x, zl, y + 1, zh, c


def down_y(x, zl, y, zh, c):
    return x, zl, y - 1, zh, c


def up_x(x, zl, y, zh, c):
    return x + 1, zl, y, zh, c


def down_x(x, zl, y, zh, c):
    return x - 1, zl, y, zh, c


def other_zh(x, zl, y, zh, c):
    return x, zl, y, 1 - zh, c


def other_core(x, zl, y, zh, c):
    return x, zl, y, zh, 1 - c


def next_zl(x, zl, y, zh, c):
    return x, LOOP[zl], y, zh, c


def last_zl(x, zl, y, zh, c):
    return x, LOOP.index(zl), y, zh, c


SPREAD = ((0, 1, 3, 2), (1, 2, 0, 3), (3, 0, 2, 1), (0, 1, 3, 2))
ORIGIN = [0, 0]
for _old, _row in enumerate(SPREAD):
    for _token, _new in enumerate(_row):
        ORIGIN[_old // 2] |= _token << 2 * (_old % 2 * 4 + _new)


def transpose(x, zl, y, zh, c):
    return x + y, SPREAD[zl][zh * 2 + c], x, zl >> 1, zl & 1


class Steps:
    def __init__(self):
        self.last = ()

    def hold(self, *values):
        if self.last:
            values = lax.optimization_barrier((*values, *self.last))[: len(values)]
        return values

    def __call__(self, *moves, slow=0):
        values = self.hold(*(value for value, _ in moves))
        results = [send(value, target) for value, (_, target) in zip(values, moves)]
        self.last = results[slow:]
        return results


def place_of():
    tp, hb = lax.axis_index("tp"), lax.axis_index("hb")
    return tp // 4, tp % 4, hb // 4, hb // 2 % 2, hb % 2


OFFSETS = (0, -1, 1, 2)


def copy_all(pairs, sems):
    copies = [
        pltpu.make_async_copy(source, target, sems.at[k])
        for k, (source, target) in enumerate(pairs)
    ]
    for copy in copies:
        copy.start()
    return copies


def rows_kernel(*refs):
    blocks, panel, sems = refs[:8], refs[8], refs[9]
    _, _, y, zh, _ = place_of()
    pairs = []
    for flip in range(2):
        for offset, block in zip(OFFSETS, blocks[4 * flip : 4 * flip + 4]):
            slot = (y + offset + 4) % 4 * 2 + (zh ^ flip)
            pairs.append((block, panel.at[slot]))
    for copy in copy_all(pairs, sems):
        copy.wait()


def rows_panel(blocks):
    return pl.pallas_call(
        rows_kernel,
        out_shape=jax.ShapeDtypeStruct((8, *blocks[0].shape), blocks[0].dtype),
        in_specs=[pl.BlockSpec(memory_space=pl.ANY)] + [VMEM] * 7,
        out_specs=VMEM,
        scratch_shapes=[pltpu.SemaphoreType.DMA((8,))],
        compiler_params=pltpu.CompilerParams(vmem_limit_bytes=4 << 20),
        cost_estimate=pl.CostEstimate(
            flops=0, bytes_accessed=1 << 20, transcendentals=0
        ),
    )(*blocks)


def in_kernel(steps, scale, *refs):
    own, other = refs[:2]
    blocks = refs[2 : 2 + 4 * len(steps)]
    left, right, tiles, sems, out_sems = refs[-5:]
    out, before = refs[-6], refs[2 + 4 * len(steps) : -6]
    x, zl, y, zh, c = place_of()
    codes = jnp.where(zh == 0, ORIGIN[0], ORIGIN[1]) >> 8 * c
    tokens = own.shape[1]
    copies = []
    for step in range(4):
        group = codes >> 2 * zl & 3
        swap = group & 1 ^ c
        for k, offset in enumerate(OFFSETS if step in steps else ()):
            at = 4 * steps.index(step) + k
            rows = pl.ds(at * tokens, tokens)
            slot = (x + offset - y + 8) % 4 * 2 + (group >> 1)
            copies.append(
                pltpu.make_async_copy(blocks[at], right.at[rows, :], sems.at[0, at])
            )
            copies[-1].start()
            near = pltpu.make_async_copy(own.at[slot], left.at[rows, :], sems.at[1, at])
            far = pltpu.make_async_copy(other.at[slot], left.at[rows, :], sems.at[1, at])
            pl.when(swap == 0)(near.start)
            pl.when(swap == 1)(far.start)
            copies.append(near)
        zl = jnp.where(zl == 0, 2, jnp.where(zl == 1, 0, jnp.where(zl == 2, 3, 1)))
    for copy in copies:
        copy.wait()
    tile = tiles.shape[1]
    writes = []
    for m in range(out.shape[0] // tile):
        at = slice(m * tile, (m + 1) * tile)
        part = scale * lax.dot_general(
            left[:, at], right[...], DOT, preferred_element_type=jnp.float32
        )
        if not before:
            out[at, :] = part
            continue
        if m > 1:
            writes[m - 2].wait()
        tiles[m % 2] = before[0][at, :] + part
        writes.append(
            pltpu.make_async_copy(tiles.at[m % 2], out.at[at, :], out_sems.at[m % 2])
        )
        writes[-1].start()
    for write in writes[-2:]:
        write.wait()


def in_product(own, other, blocks, steps, scale, before=()):
    tokens, width = blocks[0].shape
    count = len(blocks)
    return pl.pallas_call(
        functools.partial(in_kernel, steps, scale),
        out_shape=jax.ShapeDtypeStruct((width, width), jnp.float32),
        in_specs=[VMEM] * (2 + count + len(before)),
        out_specs=pl.BlockSpec(memory_space=pl.ANY) if before else VMEM,
        scratch_shapes=[
            pltpu.VMEM((count * tokens, width), jnp.bfloat16),
            pltpu.VMEM((count * tokens, width), jnp.bfloat16),
            pltpu.VMEM((2, width // 4, width), jnp.float32),
            pltpu.SemaphoreType.DMA((2, count)),
            pltpu.SemaphoreType.DMA((2,)),
        ],
        compiler_params=pltpu.CompilerParams(vmem_limit_bytes=20 << 20),
        cost_estimate=pl.CostEstimate(
            flops=2 * count * tokens * width * width,
            bytes_accessed=8 << 20,
            transcendentals=0,
        ),
    )(own, other, *blocks, *before)


def down_kernel(count, scale, *refs):
    blocks, before = refs[:count], refs[count:-4]
    mine, theirs, panel, sems = refs[-4:]
    pairs, start = [], 0
    for block in blocks:
        stop = start + block.shape[0]
        pairs.append((block, panel.at[start:stop, :]))
        start = stop
    copies = copy_all(pairs, sems)
    rows, width = mine.shape
    group = lax.axis_index("hb")
    span = 384
    base = jnp.minimum(group // 2 * 2 * rows // 128 * 128, width - span)
    base = pl.multiple_of(base, 128)
    lane = lax.broadcasted_iota(jnp.int32, (span, 256), 1)
    owner = jnp.where(lane < 128, group, group ^ 1)
    wanted = owner * rows - base + (lane & 127)
    pick = lax.broadcasted_iota(jnp.int32, (span, 256), 0) == wanted
    for copy in copies:
        copy.wait()
    left = jnp.dot(
        panel[:, pl.ds(base, span)],
        jnp.where(pick, 1.0, 0.0).astype(jnp.bfloat16),
        preferred_element_type=jnp.float32,
    ).astype(jnp.bfloat16)
    both = scale * lax.dot_general(
        left, panel[...], DOT, preferred_element_type=jnp.float32
    )
    for term, at in ((mine, 0), (theirs, 128)):
        part = both[at : at + rows]
        term[...] = part if not before else before[at // 128][...] + part


def down_terms(blocks, scale, before=()):
    width = blocks[0].shape[1]
    tokens = sum(block.shape[0] for block in blocks)
    rows = width // lax.axis_size("hb")
    term = jax.ShapeDtypeStruct((rows, width), jnp.float32)
    first = VMEM if before else pl.BlockSpec(memory_space=pl.ANY)
    return pl.pallas_call(
        functools.partial(down_kernel, len(blocks), scale),
        out_shape=(term, term),
        in_specs=[first] + [VMEM] * (len(blocks) - 1 + len(before)),
        out_specs=(VMEM, VMEM),
        scratch_shapes=[
            pltpu.VMEM((tokens, width), jnp.bfloat16),
            pltpu.SemaphoreType.DMA((len(blocks),)),
        ],
        compiler_params=pltpu.CompilerParams(vmem_limit_bytes=16 << 20),
        cost_estimate=pl.CostEstimate(
            flops=2 * tokens * 256 * width,
            bytes_accessed=6 << 20,
            transcendentals=0,
        ),
    )(*blocks, *before)


def per_device(normed, hidden):
    scale = 2.0 / (normed.shape[0] * lax.axis_size("hb"))
    step = Steps()
    first, normed_1, h_below, h_above = step(
        (normed, transpose), (normed, other_zh), (hidden, up_y), (hidden, down_y)
    )
    second, fourth, x_below_0, x_above_0, n_below, n_above = step(
        (first, next_zl), (first, last_zl), (first, up_x), (first, down_x),
        (normed, up_y), (normed, down_y)
    )
    hidden_1, third, x_below_1, x_above_1, n_below_1, n_above_1 = step(
        (hidden, other_zh), (second, next_zl), (second, up_x), (second, down_x),
        (normed_1, up_y), (normed_1, down_y), slow=1,
    )
    pair = jnp.concatenate([third, fourth], axis=0)
    x_below, x_above, n_far, n_far_1, h_far = step(
        (pair, up_x), (pair, down_x), (n_below, up_y), (n_above_1, down_y), (h_below, up_y)
    )
    tokens = normed.shape[0]
    x_below_2, x_below_3 = x_below[:tokens], x_below[tokens:]
    x_above_2, x_above_3 = x_above[:tokens], x_above[tokens:]
    own = rows_panel(
        [normed, n_below, n_above, n_far, normed_1, n_below_1, n_above_1, n_far_1]
    )
    h_below_1, h_above_1, x_far_0, x_far_1, other = step(
        (hidden_1, up_y), (hidden_1, down_y), (x_below_0, up_x), (x_above_1, down_x),
        (own, other_core)
    )
    early = [first, x_below_0, x_above_0, x_far_0, second, x_below_1, x_above_1, x_far_1]
    partial = in_product(own, other, early, (0, 1), scale)
    terms = down_terms(
        [hidden, h_below, h_above, h_far, hidden_1, h_below_1, h_above_1], scale
    )
    half = tokens // 2
    *far, x_far_2, x_far_3 = step(
        (h_above_1[:half], down_y), (h_below_1[half:], up_y),
        (x_below_2, up_x), (x_above_3, down_x)
    )
    *held, partial = step.hold(*far, partial)
    mine, theirs = down_terms(held, scale, terms)
    h_down = mine + send(theirs, other_core)
    late = [third, x_below_2, x_above_2, x_far_2, fourth, x_below_3, x_above_3, x_far_3]
    h_in = in_product(own, other, late, (2, 3), scale, (partial,))
    return (h_in, h_down)


def solution(mesh):
    return jax.shard_map(
        per_device,
        mesh=mesh,
        in_specs=(P("hb", "tp"), P("hb", "tp")),
        out_specs=(P("tp", "hb"), P(("tp", "hb"), None)),
        check_vma=False,
    )
```
